32 devices in a mesh: kset: 2 (over y), grid: 16 (over z, x, core).
Axes of the slice: x: 2, y: 2, z: 4, core: 2. Of those that a mesh axis runs over, the one named last changes fastest.
Arguments:
- bands: bfloat16 [4, 4096, 1536], P('kset', 'grid'), parts along dimension 0, may hold values from -4 to 4, as said below
- hbands: bfloat16 [4, 4096, 1536], P('kset', 'grid'), parts along dimension 0, may hold values from -10 to 10, as said below
- occupied: int32 [4], P('kset'), parts along dimension 0, may hold values from 192 to 576
Outputs:
- new_bands: bfloat16 [4, 4096, 1536], P('kset', 'grid'), parts along dimension 0
The draws below stay inside these ranges and needn't reach their ends.
There are 2 independent parts, one for each index of `kset`. The reference program is written for one: setup_inputs(seed, part) draws one part's arguments, and reference() takes and returns one part's arrays. A program takes and returns all parts, laid end to end along the dimension named above; each array names one. Nothing has to cross between parts.
Inputs may be any that keep to these rules, and one draw needn't show every extreme that they name: `bands`: real values on every grid point. `hbands`: real values on every grid point.
All inputs are finite; a program needn't handle non-finite values.
Results may differ from the reference program's by a relative error of at most 0.0079.
Values may be sent and summed in bfloat16 or wider, within the bound.
A program may use at most 64 MiB of HBM per device.

```python
import math
import jax
import jax.numpy as jnp
from jax import lax

NB = 768
KP = 2
MCW = 2
GRID = 4096


def draw_pair(key):
    band_key = jax.random.fold_in(key, 11)
    noise_key = jax.random.fold_in(key, 12)
    shape = (KP, GRID, 2 * NB)
    base = jnp.clip(jax.random.normal(band_key, shape, jnp.float32), -4.0, 4.0)
    noise = jnp.clip(jax.random.normal(noise_key, shape, jnp.float32), -4.0, 4.0)
    column = jnp.arange(2 * NB) % NB
    energy = 1.0 + 2.0 * column.astype(jnp.float32) / NB
    factor = 1.4 * math.sqrt(NB / GRID)
    applied = jnp.clip(factor * energy * base + noise, -10.0, 10.0)
    return (base, applied)


def draw_bands(key, part):
    return draw_pair(key)[0].astype(jnp.bfloat16)


def draw_hbands(key, part):
    return draw_pair(key)[1].astype(jnp.bfloat16)


def setup_inputs(seed: int = 0, part: int = 0) -> dict:
    seeds = jax.random.split(jax.random.key(seed), 4)
    part_keys = jax.random.split(jax.random.fold_in(seeds[3], part), 4)
    bands = draw_bands(jax.random.fold_in(jax.random.fold_in(seeds[3], part), 71), part)
    hbands = draw_hbands(jax.random.fold_in(jax.random.fold_in(seeds[3], part), 71), part)
    occupied = jax.random.randint(part_keys[2], (KP,), NB // 4, 3 * NB // 4 + 1).astype(jnp.int32)
    return {"bands": bands, "hbands": hbands, "occupied": occupied}


def embedding(full):
    width = full.shape[-1] // 2
    real_part = full[..., :width]
    imag_part = full[..., width:]
    upper = jnp.concatenate([real_part, imag_part], -1)
    lower = jnp.concatenate([-imag_part, real_part], -1)
    return jnp.concatenate([upper, lower], -2)

def reference(bands, hbands, occupied):
    results = []
    for point in range(KP):
        band_f = bands[point].astype(jnp.float32)
        hband_f = hbands[point].astype(jnp.float32)
        product = jnp.dot(band_f.T, hband_f, precision=lax.Precision.HIGHEST)
        real_sum = product[:NB, :NB] + product[NB:, NB:]
        imag_sum = product[:NB, NB:] - product[NB:, :NB]
        ham_real = (real_sum + real_sum.T) / (2.0 * GRID)
        ham_imag = (imag_sum - imag_sum.T) / (2.0 * GRID)
        identity = jnp.eye(NB, dtype=jnp.float32)
        level = jnp.trace(ham_real) / NB
        centred = ham_real - level * identity
        total = jnp.sum(centred * centred) + jnp.sum(ham_imag * ham_imag)
        spread = jnp.sqrt(total / NB + 1e-06)
        filling = occupied[point].astype(jnp.float32) / NB
        dens_real = filling * identity - centred / (4.0 * spread)
        dens_imag = -ham_imag / (4.0 * spread)
        density = jnp.concatenate([dens_real, dens_imag], 1).astype(jnp.bfloat16)
        for repeat in range(MCW):
            matrix = embedding(density)
            square = jnp.dot(density, matrix, preferred_element_type=jnp.float32)
            cube = jnp.dot(square.astype(jnp.bfloat16), matrix, preferred_element_type=jnp.float32)
            density = (3.0 * square - 2.0 * cube).astype(jnp.bfloat16)
        matrix = embedding(density).astype(jnp.float32)
        updated = jnp.dot(band_f, matrix, precision=lax.Precision.HIGHEST)
        results.append(updated.astype(jnp.bfloat16))
    return jnp.stack(results)
```

```python
import functools

import jax
import jax.numpy as jnp
from jax import lax
from jax.experimental import pallas as pl
from jax.experimental.pallas import tpu as pltpu
from jax.sharding import PartitionSpec as P

MCW = 2
LINE = 4
CHIPS = 2 * LINE
TILE = 256
MESH = pl.DeviceIdType.MESH


def dot_t(left, right):
    return lax.dot_general(
        left, right, (((0,), (0,)), ((), ())), preferred_element_type=jnp.float32
    )


def dot(left, right):
    return jnp.dot(left, right, preferred_element_type=jnp.float32)


def kernel(
    scale,
    occ_ref,
    bands_ref,
    hbands_ref,
    out_ref,
    rb,
    rh,
    packed,
    xs,
    xr,
    zs,
    zr,
    dl,
    dr,
    full,
    re0,
    im0,
    re1,
    im1,
    ob,
    in_send,
    in_recv,
    xs_sem,
    xr_sem,
    zs_sem,
    zr_sem,
    ds_sem,
    dr_sem,
    gzs_sem,
    gzr_sem,
    gxs_sem,
    gxr_sem,
    o_sem,
):
    rows = bands_ref.shape[1]
    half = bands_ref.shape[2] // 2
    share = half // CHIPS
    tiles = half // TILE
    kset = lax.axis_index("kset")
    me = lax.axis_index("grid")
    core = lax.rem(me, 2)
    chip = me // 2
    x = lax.rem(chip, 2)
    z = chip // 2

    def device(chip_id, core_id):
        return (kset, chip_id * 2 + core_id)

    mate = device(chip, 1 - core)
    across = device(z * 2 + 1 - x, core)

    def piece(zz, xx):
        return pl.ds(pl.multiple_of((zz * 2 + xx) * share, 16), share)

    def remote(src, dst, send, recv, target):
        return pltpu.make_async_remote_copy(
            src_ref=src,
            dst_ref=dst,
            send_sem=send,
            recv_sem=recv,
            device_id=target,
            device_id_type=MESH,
        )

    barrier = pltpu.get_barrier_semaphore()
    pl.semaphore_signal(barrier, inc=1, device_id=mate, device_id_type=MESH)
    for r in range(1, CHIPS):
        pl.semaphore_signal(
            barrier, inc=1, device_id=device(lax.rem(chip + r, CHIPS), core), device_id_type=MESH
        )
    pl.semaphore_wait(barrier, CHIPS)

    swap_b = remote(bands_ref.at[1 - core], rb, in_send.at[0], in_recv.at[0], mate)
    swap_h = remote(hbands_ref.at[1 - core], rh, in_send.at[1], in_recv.at[1], mate)
    swap_b.start()
    swap_h.start()

    def project(band, hband, first):
        for i in range(tiles):
            lo, hi = i * TILE, (i + 1) * TILE
            a_i = band[:, lo:hi]
            b_i = band[:, half + lo : half + hi]
            ha_i = hband[:, lo:hi]
            hb_i = hband[:, half + lo : half + hi]
            real = (
                dot_t(a_i, hband[:, lo:half])
                + dot_t(b_i, hband[:, half + lo :])
                + dot_t(ha_i, band[:, lo:half])
                + dot_t(hb_i, band[:, half + lo :])
            ) * scale
            imag = (
                dot_t(a_i, hband[:, half : half + hi])
                + dot_t(ha_i, band[:, half : half + hi])
                - dot_t(b_i, hband[:, :hi])
                - dot_t(hb_i, band[:, :hi])
            ) * scale
            r_id = lax.broadcasted_iota(jnp.int32, (TILE, TILE), 0)
            c_id = lax.broadcasted_iota(jnp.int32, (TILE, TILE), 1)
            square_r = real[:, :TILE]
            square_i = imag[:, lo:hi]
            diag = jnp.sum(jnp.where(r_id == c_id, square_r, 0.0), axis=0, keepdims=True)
            diag = jnp.broadcast_to(diag, (8, TILE))
            mixed = jnp.where(r_id < c_id, square_r, jnp.where(r_id > c_id, square_i, 0.0))
            pieces = [(lo, hi, mixed)]
            if lo > 0:
                pieces.append((0, lo, imag[:, :lo]))
            if hi < half:
                pieces.append((hi, half, real[:, TILE:]))
            for c0, c1, value in pieces:
                if first:
                    packed[lo:hi, c0:c1] = value
                else:
                    packed[lo:hi, c0:c1] = packed[lo:hi, c0:c1] + value
            if first:
                dl[:, lo:hi] = diag
            else:
                dl[:, lo:hi] = dl[:, lo:hi] + diag

    project(bands_ref.at[core], hbands_ref.at[core], True)
    swap_b.wait()
    swap_h.wait()
    project(rb, rh, False)

    swaps = {}
    for d in (1, 2, 3, 0):
        q = lax.rem(z + d, LINE)
        xs[d] = packed[piece(q, 1 - x), :].astype(jnp.bfloat16)
        swaps[d] = remote(xs.at[d], xr.at[d], xs_sem.at[d], xr_sem.at[d], across)
        swaps[d].start()
    traces = []
    for r in range(1, CHIPS):
        copy = remote(
            dl,
            dr.at[r - 1],
            ds_sem.at[r - 1],
            dr_sem.at[r - 1],
            device(lax.rem(chip + r, CHIPS), core),
        )
        copy.start()
        traces.append(copy)
    sums = []
    for d in range(1, LINE):
        q = lax.rem(z + d, LINE)
        swaps[d].wait()
        zs[d - 1] = (packed[piece(q, x), :] + xr[d].astype(jnp.float32)).astype(jnp.bfloat16)
        copy = remote(
            zs.at[d - 1], zr.at[d - 1], zs_sem.at[d - 1], zr_sem.at[d - 1], device(q * 2 + x, core)
        )
        copy.start()
        sums.append(copy)
    swaps[0].wait()
    mine = packed[piece(z, x), :] + xr[0].astype(jnp.float32)
    for d in range(1, LINE):
        sums[d - 1].wait()
        mine = mine + zr[d - 1].astype(jnp.float32)
    own = piece(z, x)
    full[own, :] = mine.astype(jnp.bfloat16)

    gathers = []
    for d in range(1, LINE):
        copy = remote(
            full.at[own, :],
            full.at[own, :],
            gzs_sem.at[d - 1],
            gzr_sem.at[d - 1],
            device(lax.rem(z + d, LINE) * 2 + x, core),
        )
        copy.start()
        gathers.append(copy)
    passes = [
        remote(full.at[own, :], full.at[own, :], gxs_sem.at[0], gxr_sem.at[0], across)
    ]
    passes[0].start()
    for d in range(1, LINE):
        gathers[d - 1].wait_recv()
        theirs = piece(lax.rem(z - d + LINE, LINE), x)
        copy = remote(full.at[theirs, :], full.at[theirs, :], gxs_sem.at[d], gxr_sem.at[d], across)
        copy.start()
        passes.append(copy)
    diag = dl[...]
    for r in range(1, CHIPS):
        traces[r - 1].wait()
        diag = diag + dr[r - 1]
    diag = diag[0:1, :]
    for copy in gathers:
        copy.wait_send()
    for copy in passes:
        copy.wait()

    level = jnp.sum(diag, axis=1, keepdims=True) / half
    centred = diag - level
    total = jnp.sum(centred * centred, axis=1, keepdims=True)
    square_sum = jnp.zeros((1, half), jnp.float32)
    for i in range(tiles):
        block = full[i * TILE : (i + 1) * TILE, :].astype(jnp.float32)
        square_sum = square_sum + jnp.sum(block * block, axis=0, keepdims=True)
    total = total + 2.0 * jnp.sum(square_sum, axis=1, keepdims=True)
    spread = jnp.sqrt(total / half + 1e-06)
    factor = 1.0 / (4.0 * spread)
    filling = occ_ref[core].astype(jnp.float32) / half
    on_diag = filling - centred * factor
    for i in range(tiles):
        si = slice(i * TILE, (i + 1) * TILE)
        r_id = lax.broadcasted_iota(jnp.int32, (TILE, TILE), 0)
        c_id = lax.broadcasted_iota(jnp.int32, (TILE, TILE), 1)
        block = full[si, si].astype(jnp.float32) * factor
        turned = block.T
        re0[si, si] = jnp.where(
            r_id == c_id, on_diag[:, si], jnp.where(r_id < c_id, -block, -turned)
        ).astype(jnp.bfloat16)
        im0[si, si] = jnp.where(r_id > c_id, -block, turned).astype(jnp.bfloat16)
        for j in range(i + 1, tiles):
            sj = slice(j * TILE, (j + 1) * TILE)
            upper = full[si, sj].astype(jnp.float32) * factor
            lower = full[sj, si].astype(jnp.float32) * factor
            re0[si, sj] = (-upper).astype(jnp.bfloat16)
            re0[sj, si] = (-upper.T).astype(jnp.bfloat16)
            im0[sj, si] = (-lower).astype(jnp.bfloat16)
            im0[si, sj] = lower.T.astype(jnp.bfloat16)

    def purify(re, im, re_next, im_next):
        def body(i, carry):
            block = pl.ds(pl.multiple_of(i * TILE, TILE), TILE)
            r_i, i_i = re[block, :], im[block, :]
            sq_r = dot(r_i, re[...]) - dot(i_i, im[...])
            sq_i = dot(r_i, im[...]) + dot(i_i, re[...])
            s_r, s_i = sq_r.astype(jnp.bfloat16), sq_i.astype(jnp.bfloat16)
            cu_r = dot(s_r, re[...]) - dot(s_i, im[...])
            cu_i = dot(s_r, im[...]) + dot(s_i, re[...])
            re_next[block, :] = (3.0 * sq_r - 2.0 * cu_r).astype(jnp.bfloat16)
            im_next[block, :] = (3.0 * sq_i - 2.0 * cu_i).astype(jnp.bfloat16)
            return carry

        lax.fori_loop(0, tiles, body, 0)

    bufs = [(re0, im0), (re1, im1)]
    for step in range(MCW):
        purify(*bufs[step % 2], *bufs[(step + 1) % 2])
    re, im = bufs[MCW % 2]

    def update(band, target):
        a, b = band[:, :half], band[:, half:]
        target[:, :half] = (dot(a, re[...]) - dot(b, im[...])).astype(jnp.bfloat16)
        target[:, half:] = (dot(a, im[...]) + dot(b, re[...])).astype(jnp.bfloat16)

    update(rb, ob)
    back = remote(ob, out_ref.at[core], o_sem.at[0], o_sem.at[1], mate)
    back.start()
    update(bands_ref.at[core], out_ref.at[core])
    back.wait()


def fused(bands, hbands, occupied):
    points, rows, columns = bands.shape
    half = columns // 2
    share = half // CHIPS
    scale = 1.0 / (2.0 * rows * lax.axis_size("grid"))
    bf16, f32 = jnp.bfloat16, jnp.float32
    dma = pltpu.SemaphoreType.DMA
    return pl.pallas_call(
        functools.partial(kernel, scale),
        out_shape=jax.ShapeDtypeStruct(bands.shape, bf16),
        in_specs=[
            pl.BlockSpec(memory_space=pltpu.SMEM),
            pl.BlockSpec(memory_space=pltpu.VMEM),
            pl.BlockSpec(memory_space=pltpu.VMEM),
        ],
        out_specs=pl.BlockSpec(memory_space=pltpu.VMEM),
        scratch_shapes=[
            pltpu.VMEM((rows, columns), bf16),
            pltpu.VMEM((rows, columns), bf16),
            pltpu.VMEM((half, half), f32),
            pltpu.VMEM((LINE, share, half), bf16),
            pltpu.VMEM((LINE, share, half), bf16),
            pltpu.VMEM((LINE - 1, share, half), bf16),
            pltpu.VMEM((LINE - 1, share, half), bf16),
            pltpu.VMEM((8, half), f32),
            pltpu.VMEM((CHIPS - 1, 8, half), f32),
            pltpu.VMEM((half, half), bf16),
            pltpu.VMEM((half, half), bf16),
            pltpu.VMEM((half, half), bf16),
            pltpu.VMEM((half, half), bf16),
            pltpu.VMEM((half, half), bf16),
            pltpu.VMEM((rows, columns), bf16),
            dma((2,)),
            dma((2,)),
            dma((LINE,)),
            dma((LINE,)),
            dma((LINE - 1,)),
            dma((LINE - 1,)),
            dma((CHIPS - 1,)),
            dma((CHIPS - 1,)),
            dma((LINE - 1,)),
            dma((LINE - 1,)),
            dma((LINE,)),
            dma((LINE,)),
            dma((2,)),
        ],
        compiler_params=pltpu.CompilerParams(
            collective_id=0, has_side_effects=True, vmem_limit_bytes=50 * 1024 * 1024
        ),
    )(occupied, bands, hbands)


def embedding(full):
    width = full.shape[-1] // 2
    real_part = full[..., :width]
    imag_part = full[..., width:]
    upper = jnp.concatenate([real_part, imag_part], -1)
    lower = jnp.concatenate([-imag_part, real_part], -1)
    return jnp.concatenate([upper, lower], -2)


def spread_out(bands, hbands, occupied):
    points, local_rows, columns = bands.shape
    half = columns // 2
    devices = lax.axis_size("grid")
    share = half // devices
    scale = 1.0 / (2.0 * local_rows * devices)
    blocks = []
    for point in range(points):
        start = jnp.int32(0)
        count = lax.axis_size("grid") * share
        band_k = bands[point]
        hband_k = hbands[point]
        band_cols = jnp.concatenate(
            [
                lax.dynamic_slice_in_dim(band_k, start, count, 1),
                lax.dynamic_slice_in_dim(band_k, half, count, 1),
            ],
            1,
        )
        summed = jnp.einsum("gi,gj->ij", band_cols, hband_k, preferred_element_type=jnp.float32)
        hband_cols = jnp.concatenate(
            [
                lax.dynamic_slice_in_dim(hband_k, start, count, 1),
                lax.dynamic_slice_in_dim(hband_k, half, count, 1),
            ],
            1,
        )
        summed = summed + jnp.einsum(
            "gi,gj->ij", hband_cols, band_k, preferred_element_type=jnp.float32
        )
        real_rows = (summed[:count, :half] + summed[count:, half:]) * scale
        imag_rows = (summed[:count, half:] - summed[count:, :half]) * scale
        blocks.append(
            lax.psum_scatter(
                jnp.concatenate([real_rows, imag_rows], 1), "grid", scatter_dimension=0, tiled=True
            )
        )
    hamiltonian = jnp.stack(blocks, 1)
    hamiltonian = jnp.transpose(hamiltonian, (1, 0, 2))
    ham_real = hamiltonian[:, :, :half]
    ham_imag = hamiltonian[:, :, half:]
    row_index = lax.axis_index("grid") * share + lax.iota(jnp.int32, share)
    col_index = lax.iota(jnp.int32, half)
    identity = (row_index[:, None] == col_index[None, :]).astype(jnp.float32)[None]
    trace_part = jnp.sum(ham_real * identity, axis=(1, 2))
    trace = lax.psum(trace_part, "grid")
    level = (trace / half)[:, None, None]
    centred = ham_real - level * identity
    squares = jnp.sum(centred * centred, axis=(1, 2)) + jnp.sum(ham_imag * ham_imag, axis=(1, 2))
    total = lax.psum(squares, "grid")
    spread = jnp.sqrt(total / half + 1e-06)[:, None, None]
    filling = (occupied.astype(jnp.float32) / half)[:, None, None]
    dens_real = filling * identity - centred / (4.0 * spread)
    dens_imag = -ham_imag / (4.0 * spread)
    density = jnp.concatenate([dens_real, dens_imag], 2).astype(jnp.bfloat16)
    for repeat in range(MCW):
        gathered = lax.all_gather(density, "grid", axis=1, tiled=True)
        matrix = embedding(gathered)
        square = jnp.einsum("krc,kcd->krd", density, matrix, preferred_element_type=jnp.float32)
        cube = jnp.einsum(
            "krc,kcd->krd", square.astype(jnp.bfloat16), matrix, preferred_element_type=jnp.float32
        )
        density = (3.0 * square - 2.0 * cube).astype(jnp.bfloat16)
    gathered = lax.all_gather(density, "grid", axis=1, tiled=True)
    matrix = embedding(gathered)
    updated = jnp.einsum("kgc,kcd->kgd", bands, matrix, preferred_element_type=jnp.float32)
    return updated.astype(jnp.bfloat16)


def on_device(bands, hbands, occupied):
    points, rows, columns = bands.shape
    half = columns // 2
    if (
        lax.axis_size("grid") == 2 * CHIPS
        and points == 2
        and half % TILE == 0
        and half % (16 * CHIPS) == 0
    ):
        return fused(bands, hbands, occupied)
    return spread_out(bands, hbands, occupied)


def solution(mesh):
    return jax.shard_map(
        on_device,
        mesh=mesh,
        in_specs=(P("kset", "grid", None), P("kset", "grid", None), P("kset")),
        out_specs=P("kset", "grid", None),
        check_vma=False,
    )
```

```python
import functools

import jax
import jax.numpy as jnp
from jax import lax
from jax.experimental import pallas as pl
from jax.experimental.pallas import tpu as pltpu
from jax.sharding import PartitionSpec as P

MCW = 2
LINE = 4
CHIPS = 2 * LINE
TILE = 256
MESH = pl.DeviceIdType.MESH


def dot_t(left, right):
    return lax.dot_general(
        left, right, (((0,), (0,)), ((), ())), preferred_element_type=jnp.float32
    )


def dot(left, right):
    return jnp.dot(left, right, preferred_element_type=jnp.float32)


def kernel(
    scale,
    occ_ref,
    bands_ref,
    hbands_ref,
    out_ref,
    rb,
    rh,
    packed,
    xs,
    xr,
    ls,
    lr,
    ws,
    wr,
    dl,
    dr,
    full,
    re0,
    im0,
    re1,
    im1,
    ob,
    in_send,
    in_recv,
    xs_sem,
    xr_sem,
    zs_sem,
    zr_sem,
    ds_sem,
    dr_sem,
    gzs_sem,
    gzr_sem,
    gxs_sem,
    gxr_sem,
    o_sem,
):
    rows = bands_ref.shape[1]
    half = bands_ref.shape[2] // 2
    share = half // CHIPS
    tiles = half // TILE
    kset = lax.axis_index("kset")
    me = lax.axis_index("grid")
    core = lax.rem(me, 2)
    chip = me // 2
    x = lax.rem(chip, 2)
    z = chip // 2

    def device(chip_id, core_id):
        return (kset, chip_id * 2 + core_id)

    mate = device(chip, 1 - core)
    across = device(z * 2 + 1 - x, core)

    def piece(zz, xx):
        return pl.ds(pl.multiple_of((zz * 2 + xx) * share, 16), share)

    def remote(src, dst, send, recv, target):
        return pltpu.make_async_remote_copy(
            src_ref=src,
            dst_ref=dst,
            send_sem=send,
            recv_sem=recv,
            device_id=target,
            device_id_type=MESH,
        )

    barrier = pltpu.get_barrier_semaphore()
    pl.semaphore_signal(barrier, inc=1, device_id=mate, device_id_type=MESH)
    for r in range(1, CHIPS):
        pl.semaphore_signal(
            barrier, inc=1, device_id=device(lax.rem(chip + r, CHIPS), core), device_id_type=MESH
        )
    pl.semaphore_wait(barrier, CHIPS)

    swap_b = remote(bands_ref.at[1 - core], rb, in_send.at[0], in_recv.at[0], mate)
    swap_h = remote(hbands_ref.at[1 - core], rh, in_send.at[1], in_recv.at[1], mate)
    swap_b.start()
    swap_h.start()

    def project(band, hband, first):
        for i in range(tiles):
            lo, hi = i * TILE, (i + 1) * TILE
            a_i = band[:, lo:hi]
            b_i = band[:, half + lo : half + hi]
            ha_i = hband[:, lo:hi]
            hb_i = hband[:, half + lo : half + hi]
            real = (
                dot_t(a_i, hband[:, lo:half])
                + dot_t(b_i, hband[:, half + lo :])
                + dot_t(ha_i, band[:, lo:half])
                + dot_t(hb_i, band[:, half + lo :])
            ) * scale
            imag = (
                dot_t(a_i, hband[:, half : half + hi])
                + dot_t(ha_i, band[:, half : half + hi])
                - dot_t(b_i, hband[:, :hi])
                - dot_t(hb_i, band[:, :hi])
            ) * scale
            r_id = lax.broadcasted_iota(jnp.int32, (TILE, TILE), 0)
            c_id = lax.broadcasted_iota(jnp.int32, (TILE, TILE), 1)
            square_r = real[:, :TILE]
            square_i = imag[:, lo:hi]
            diag = jnp.sum(jnp.where(r_id == c_id, square_r, 0.0), axis=0, keepdims=True)
            diag = jnp.broadcast_to(diag, (8, TILE))
            mixed = jnp.where(r_id < c_id, square_r, jnp.where(r_id > c_id, square_i, 0.0))
            pieces = [(lo, hi, mixed)]
            if lo > 0:
                pieces.append((0, lo, imag[:, :lo]))
            if hi < half:
                pieces.append((hi, half, real[:, TILE:]))
            for c0, c1, value in pieces:
                if first:
                    packed[lo:hi, c0:c1] = value
                else:
                    packed[lo:hi, c0:c1] = packed[lo:hi, c0:c1] + value
            if first:
                dl[:, lo:hi] = diag
            else:
                dl[:, lo:hi] = dl[:, lo:hi] + diag

    project(bands_ref.at[core], hbands_ref.at[core], True)
    swap_b.wait()
    swap_h.wait()
    project(rb, rh, False)

    cut = half // 2
    lefts, rights = pl.ds(0, cut), pl.ds(cut, cut)
    down = (z, LINE - 1 - z)
    ahead = (
        device((z + 1) * 2 + x, core),
        device((z - 1) * 2 + x, core),
    )

    def pair(zz):
        return pl.ds(pl.multiple_of(zz * 2 * share, 32), 2 * share)

    def across_copy(zz):
        return remote(xs.at[zz], xr.at[zz], xs_sem.at[zz], xr_sem.at[zz], across)

    for zz in (3, 0, 2, 1):
        xs[zz] = packed[piece(zz, 1 - x), lefts].astype(jnp.bfloat16)
        across_copy(zz).start()
    traces = []
    for r in range(1, CHIPS):
        copy = remote(
            dl,
            dr.at[r - 1],
            ds_sem.at[r - 1],
            dr_sem.at[r - 1],
            device(lax.rem(chip + r, CHIPS), core),
        )
        copy.start()
        traces.append(copy)

    def hop(part, way, goal):
        source, landing = ((ls, lr), (ws, wr))[part]
        slot = (part * 2 + way) * (LINE - 1) + goal - 1
        at = way * (LINE - 1) + goal - 1
        return remote(source.at[at], landing.at[at], zs_sem.at[slot], zr_sem.at[slot], ahead[way])

    def region(part, way, goal):
        zz = goal if way == 0 else LINE - 1 - goal
        return (piece(zz, x), lefts) if part == 0 else (pair(zz), rights)

    def pass_on(part, way, goal):
        source, landing = ((ls, lr), (ws, wr))[part]
        at = way * (LINE - 1) + goal - 1
        rows_at, cols_at = region(part, way, goal)
        t = down[way]

        @pl.when(t == 0)
        def _():
            source[at] = packed[rows_at, cols_at].astype(jnp.bfloat16)

        @pl.when((t > 0) & (t < goal))
        def _():
            hop(part, way, goal).wait_recv()
            source[at] = (packed[rows_at, cols_at] + landing[at].astype(jnp.float32)).astype(
                jnp.bfloat16
            )

        @pl.when(t < goal)
        def _():
            hop(part, way, goal).start()

    def land(part, way, goal):
        landing = (lr, wr)[part]
        at = way * (LINE - 1) + goal - 1
        rows_at, cols_at = region(part, way, goal)

        @pl.when(down[way] == goal)
        def _():
            hop(part, way, goal).wait_recv()
            packed[rows_at, cols_at] = packed[rows_at, cols_at] + landing[at].astype(jnp.float32)

    met = set()
    for goal in range(LINE - 1, 0, -1):
        for way in (0, 1):
            pass_on(1, way, goal)
        for zz in (goal, LINE - 1 - goal):
            if zz not in met:
                met.add(zz)
                across_copy(zz).wait()
                at = (piece(zz, x), lefts)
                packed[at] = packed[at] + xr[zz].astype(jnp.float32)
        for way in (0, 1):
            pass_on(0, way, goal)
    for goal in range(LINE - 1, 0, -1):
        for way in (0, 1):
            land(1, way, goal)
    xs[LINE] = packed[piece(z, 1 - x), rights].astype(jnp.bfloat16)
    across_copy(LINE).start()
    for goal in range(LINE - 1, 0, -1):
        for way in (0, 1):
            land(0, way, goal)
    own = piece(z, x)
    full[own, lefts] = packed[own, lefts].astype(jnp.bfloat16)

    def walk(part, way, step, source):
        zz = source if way == 0 else LINE - 1 - source
        region_at = full.at[piece(zz, x), lefts] if part == 0 else full.at[pair(zz), rights]
        slot = (part * 2 + way) * (LINE - 1) + step - 1
        return remote(region_at, region_at, gzs_sem.at[slot], gzr_sem.at[slot], ahead[way])

    def walk_send(part, way, step):
        t = down[way]
        return (t < LINE - 1) & (t >= step - 1), walk(part, way, step, t - step + 1)

    def walk_recv(part, way, step):
        t = down[way]
        return t >= step, walk(part, way, step, t - step)

    def share_x(way, step):
        zz = z if step == 0 else (z - step if way == 0 else z + step)
        region_at = full.at[piece(zz, x), lefts]
        slot = 0 if step == 0 else way * (LINE - 1) + step
        return remote(region_at, region_at, gxs_sem.at[slot], gxr_sem.at[slot], across)

    def start_walk(part, step):
        for way in (0, 1):
            go, copy = walk_send(part, way, step)
            pl.when(go)(copy.start)

    start_walk(0, 1)
    across_copy(LINE).wait()
    full[own, rights] = (packed[own, rights] + xr[LINE].astype(jnp.float32)).astype(jnp.bfloat16)
    wide = full.at[own, rights]
    last = 2 * LINE - 1
    wide_x = remote(wide, wide, gxs_sem.at[last], gxr_sem.at[last], across)
    wide_x.start()
    share_x(0, 0).start()
    wide_x.wait()
    start_walk(1, 1)
    for step in range(1, LINE):
        for part in (0, 1):
            for way in (0, 1):
                come, arriving = walk_recv(part, way, step)
                pl.when(come)(arriving.wait_recv)
                if step + 1 < LINE:
                    go, copy = walk_send(part, way, step + 1)
                    pl.when(go)(copy.start)
                if part == 0:
                    pl.when(come)(share_x(way, step).start)
    for goal in range(1, LINE):
        for part in (0, 1):
            for way in (0, 1):
                pl.when(down[way] < goal)(hop(part, way, goal).wait_send)
    diag = dl[...]
    for r in range(1, CHIPS):
        traces[r - 1].wait()
        diag = diag + dr[r - 1]
    diag = diag[0:1, :]
    for step in range(1, LINE):
        for part in (0, 1):
            for way in (0, 1):
                go, copy = walk_send(part, way, step)
                pl.when(go)(copy.wait_send)
    share_x(0, 0).wait()
    for step in range(1, LINE):
        for way in (0, 1):
            pl.when(down[way] >= step)(share_x(way, step).wait)

    level = jnp.sum(diag, axis=1, keepdims=True) / half
    centred = diag - level
    total = jnp.sum(centred * centred, axis=1, keepdims=True)
    square_sum = jnp.zeros((1, half), jnp.float32)
    for i in range(tiles):
        block = full[i * TILE : (i + 1) * TILE, :].astype(jnp.float32)
        square_sum = square_sum + jnp.sum(block * block, axis=0, keepdims=True)
    total = total + 2.0 * jnp.sum(square_sum, axis=1, keepdims=True)
    spread = jnp.sqrt(total / half + 1e-06)
    factor = 1.0 / (4.0 * spread)
    filling = occ_ref[core].astype(jnp.float32) / half
    on_diag = filling - centred * factor
    for i in range(tiles):
        si = slice(i * TILE, (i + 1) * TILE)
        r_id = lax.broadcasted_iota(jnp.int32, (TILE, TILE), 0)
        c_id = lax.broadcasted_iota(jnp.int32, (TILE, TILE), 1)
        block = full[si, si].astype(jnp.float32) * factor
        turned = block.T
        re0[si, si] = jnp.where(
            r_id == c_id, on_diag[:, si], jnp.where(r_id < c_id, -block, -turned)
        ).astype(jnp.bfloat16)
        im0[si, si] = jnp.where(r_id > c_id, -block, turned).astype(jnp.bfloat16)
        for j in range(i + 1, tiles):
            sj = slice(j * TILE, (j + 1) * TILE)
            upper = full[si, sj].astype(jnp.float32) * factor
            lower = full[sj, si].astype(jnp.float32) * factor
            re0[si, sj] = (-upper).astype(jnp.bfloat16)
            re0[sj, si] = (-upper.T).astype(jnp.bfloat16)
            im0[sj, si] = (-lower).astype(jnp.bfloat16)
            im0[si, sj] = lower.T.astype(jnp.bfloat16)

    def purify(re, im, re_next, im_next):
        def body(i, carry):
            block = pl.ds(pl.multiple_of(i * TILE, TILE), TILE)
            r_i, i_i = re[block, :], im[block, :]
            sq_r = dot(r_i, re[...]) - dot(i_i, im[...])
            sq_i = dot(r_i, im[...]) + dot(i_i, re[...])
            s_r, s_i = sq_r.astype(jnp.bfloat16), sq_i.astype(jnp.bfloat16)
            cu_r = dot(s_r, re[...]) - dot(s_i, im[...])
            cu_i = dot(s_r, im[...]) + dot(s_i, re[...])
            re_next[block, :] = (3.0 * sq_r - 2.0 * cu_r).astype(jnp.bfloat16)
            im_next[block, :] = (3.0 * sq_i - 2.0 * cu_i).astype(jnp.bfloat16)
            return carry

        lax.fori_loop(0, tiles, body, 0)

    bufs = [(re0, im0), (re1, im1)]
    for step in range(MCW):
        purify(*bufs[step % 2], *bufs[(step + 1) % 2])
    re, im = bufs[MCW % 2]

    def update(band, target):
        a, b = band[:, :half], band[:, half:]
        target[:, :half] = (dot(a, re[...]) - dot(b, im[...])).astype(jnp.bfloat16)
        target[:, half:] = (dot(a, im[...]) + dot(b, re[...])).astype(jnp.bfloat16)

    update(rb, ob)
    back = remote(ob, out_ref.at[core], o_sem.at[0], o_sem.at[1], mate)
    back.start()
    update(bands_ref.at[core], out_ref.at[core])
    back.wait()


def fused(bands, hbands, occupied):
    points, rows, columns = bands.shape
    half = columns // 2
    share = half // CHIPS
    scale = 1.0 / (2.0 * rows * lax.axis_size("grid"))
    bf16, f32 = jnp.bfloat16, jnp.float32
    dma = pltpu.SemaphoreType.DMA
    return pl.pallas_call(
        functools.partial(kernel, scale),
        out_shape=jax.ShapeDtypeStruct(bands.shape, bf16),
        in_specs=[
            pl.BlockSpec(memory_space=pltpu.SMEM),
            pl.BlockSpec(memory_space=pltpu.VMEM),
            pl.BlockSpec(memory_space=pltpu.VMEM),
        ],
        out_specs=pl.BlockSpec(memory_space=pltpu.VMEM),
        scratch_shapes=[
            pltpu.VMEM((rows, columns), bf16),
            pltpu.VMEM((rows, columns), bf16),
            pltpu.VMEM((half, half), f32),
            pltpu.VMEM((LINE + 1, share, half // 2), bf16),
            pltpu.VMEM((LINE + 1, share, half // 2), bf16),
            pltpu.VMEM((2 * (LINE - 1), share, half // 2), bf16),
            pltpu.VMEM((2 * (LINE - 1), share, half // 2), bf16),
            pltpu.VMEM((2 * (LINE - 1), 2 * share, half // 2), bf16),
            pltpu.VMEM((2 * (LINE - 1), 2 * share, half // 2), bf16),
            pltpu.VMEM((8, half), f32),
            pltpu.VMEM((CHIPS - 1, 8, half), f32),
            pltpu.VMEM((half, half), bf16),
            pltpu.VMEM((half, half), bf16),
            pltpu.VMEM((half, half), bf16),
            pltpu.VMEM((half, half), bf16),
            pltpu.VMEM((half, half), bf16),
            pltpu.VMEM((rows, columns), bf16),
            dma((2,)),
            dma((2,)),
            dma((LINE + 1,)),
            dma((LINE + 1,)),
            dma((4 * (LINE - 1),)),
            dma((4 * (LINE - 1),)),
            dma((CHIPS - 1,)),
            dma((CHIPS - 1,)),
            dma((4 * (LINE - 1),)),
            dma((4 * (LINE - 1),)),
            dma((2 * LINE,)),
            dma((2 * LINE,)),
            dma((2,)),
        ],
        compiler_params=pltpu.CompilerParams(
            collective_id=0, has_side_effects=True, vmem_limit_bytes=50 * 1024 * 1024
        ),
    )(occupied, bands, hbands)


def embedding(full):
    width = full.shape[-1] // 2
    real_part = full[..., :width]
    imag_part = full[..., width:]
    upper = jnp.concatenate([real_part, imag_part], -1)
    lower = jnp.concatenate([-imag_part, real_part], -1)
    return jnp.concatenate([upper, lower], -2)


def spread_out(bands, hbands, occupied):
    points, local_rows, columns = bands.shape
    half = columns // 2
    devices = lax.axis_size("grid")
    share = half // devices
    scale = 1.0 / (2.0 * local_rows * devices)
    blocks = []
    for point in range(points):
        start = jnp.int32(0)
        count = lax.axis_size("grid") * share
        band_k = bands[point]
        hband_k = hbands[point]
        band_cols = jnp.concatenate(
            [
                lax.dynamic_slice_in_dim(band_k, start, count, 1),
                lax.dynamic_slice_in_dim(band_k, half, count, 1),
            ],
            1,
        )
        summed = jnp.einsum("gi,gj->ij", band_cols, hband_k, preferred_element_type=jnp.float32)
        hband_cols = jnp.concatenate(
            [
                lax.dynamic_slice_in_dim(hband_k, start, count, 1),
                lax.dynamic_slice_in_dim(hband_k, half, count, 1),
            ],
            1,
        )
        summed = summed + jnp.einsum(
            "gi,gj->ij", hband_cols, band_k, preferred_element_type=jnp.float32
        )
        real_rows = (summed[:count, :half] + summed[count:, half:]) * scale
        imag_rows = (summed[:count, half:] - summed[count:, :half]) * scale
        blocks.append(
            lax.psum_scatter(
                jnp.concatenate([real_rows, imag_rows], 1), "grid", scatter_dimension=0, tiled=True
            )
        )
    hamiltonian = jnp.stack(blocks, 1)
    hamiltonian = jnp.transpose(hamiltonian, (1, 0, 2))
    ham_real = hamiltonian[:, :, :half]
    ham_imag = hamiltonian[:, :, half:]
    row_index = lax.axis_index("grid") * share + lax.iota(jnp.int32, share)
    col_index = lax.iota(jnp.int32, half)
    identity = (row_index[:, None] == col_index[None, :]).astype(jnp.float32)[None]
    trace_part = jnp.sum(ham_real * identity, axis=(1, 2))
    trace = lax.psum(trace_part, "grid")
    level = (trace / half)[:, None, None]
    centred = ham_real - level * identity
    squares = jnp.sum(centred * centred, axis=(1, 2)) + jnp.sum(ham_imag * ham_imag, axis=(1, 2))
    total = lax.psum(squares, "grid")
    spread = jnp.sqrt(total / half + 1e-06)[:, None, None]
    filling = (occupied.astype(jnp.float32) / half)[:, None, None]
    dens_real = filling * identity - centred / (4.0 * spread)
    dens_imag = -ham_imag / (4.0 * spread)
    density = jnp.concatenate([dens_real, dens_imag], 2).astype(jnp.bfloat16)
    for repeat in range(MCW):
        gathered = lax.all_gather(density, "grid", axis=1, tiled=True)
        matrix = embedding(gathered)
        square = jnp.einsum("krc,kcd->krd", density, matrix, preferred_element_type=jnp.float32)
        cube = jnp.einsum(
            "krc,kcd->krd", square.astype(jnp.bfloat16), matrix, preferred_element_type=jnp.float32
        )
        density = (3.0 * square - 2.0 * cube).astype(jnp.bfloat16)
    gathered = lax.all_gather(density, "grid", axis=1, tiled=True)
    matrix = embedding(gathered)
    updated = jnp.einsum("kgc,kcd->kgd", bands, matrix, preferred_element_type=jnp.float32)
    return updated.astype(jnp.bfloat16)


def on_device(bands, hbands, occupied):
    points, rows, columns = bands.shape
    half = columns // 2
    if (
        lax.axis_size("grid") == 2 * CHIPS
        and points == 2
        and half % TILE == 0
        and half % (16 * CHIPS) == 0
    ):
        return fused(bands, hbands, occupied)
    return spread_out(bands, hbands, occupied)


def solution(mesh):
    return jax.shard_map(
        on_device,
        mesh=mesh,
        in_specs=(P("kset", "grid", None), P("kset", "grid", None), P("kset")),
        out_specs=P("kset", "grid", None),
        check_vma=False,
    )
```

```python
import functools

import jax
import jax.numpy as jnp
from jax import lax
from jax.experimental import pallas as pl
from jax.experimental.pallas import tpu as pltpu
from jax.sharding import PartitionSpec as P

MCW = 2
LINE = 4
CHIPS = 2 * LINE
TILE = 256
MESH = pl.DeviceIdType.MESH


def dot_t(left, right):
    return lax.dot_general(
        left, right, (((0,), (0,)), ((), ())), preferred_element_type=jnp.float32
    )


def dot(left, right):
    return jnp.dot(left, right, preferred_element_type=jnp.float32)


def kernel(
    scale,
    occ_ref,
    bands_ref,
    hbands_ref,
    out_ref,
    rb,
    rh,
    packed,
    xs,
    xr,
    zs,
    zr,
    dl,
    dr,
    full,
    re0,
    im0,
    re1,
    im1,
    sr,
    si,
    ob,
    in_send,
    in_recv,
    xs_sem,
    xr_sem,
    zs_sem,
    zr_sem,
    ds_sem,
    dr_sem,
    gzs_sem,
    gzr_sem,
    gxs_sem,
    gxr_sem,
    o_sem,
):
    rows = bands_ref.shape[1]
    half = bands_ref.shape[2] // 2
    share = half // CHIPS
    tiles = half // TILE
    kset = lax.axis_index("kset")
    me = lax.axis_index("grid")
    core = lax.rem(me, 2)
    chip = me // 2
    x = lax.rem(chip, 2)
    z = chip // 2

    def device(chip_id, core_id):
        return (kset, chip_id * 2 + core_id)

    mate = device(chip, 1 - core)
    across = device(z * 2 + 1 - x, core)

    def piece(zz, xx):
        return pl.ds(pl.multiple_of((zz * 2 + xx) * share, 16), share)

    def remote(src, dst, send, recv, target):
        return pltpu.make_async_remote_copy(
            src_ref=src,
            dst_ref=dst,
            send_sem=send,
            recv_sem=recv,
            device_id=target,
            device_id_type=MESH,
        )

    barrier = pltpu.get_barrier_semaphore()
    pl.semaphore_signal(barrier, inc=1, device_id=mate, device_id_type=MESH)
    for r in range(1, CHIPS):
        pl.semaphore_signal(
            barrier, inc=1, device_id=device(lax.rem(chip + r, CHIPS), core), device_id_type=MESH
        )
    pl.semaphore_wait(barrier, CHIPS)

    swap_b = remote(bands_ref.at[1 - core], rb, in_send.at[0], in_recv.at[0], mate)
    swap_h = remote(hbands_ref.at[1 - core], rh, in_send.at[1], in_recv.at[1], mate)
    swap_b.start()
    swap_h.start()

    def project(band, hband, first):
        for i in range(tiles):
            lo, hi = i * TILE, (i + 1) * TILE
            a_i = band[:, lo:hi]
            b_i = band[:, half + lo : half + hi]
            ha_i = hband[:, lo:hi]
            hb_i = hband[:, half + lo : half + hi]
            real = (
                dot_t(a_i, hband[:, lo:half])
                + dot_t(b_i, hband[:, half + lo :])
                + dot_t(ha_i, band[:, lo:half])
                + dot_t(hb_i, band[:, half + lo :])
            ) * scale
            imag = (
                dot_t(a_i, hband[:, half : half + hi])
                + dot_t(ha_i, band[:, half : half + hi])
                - dot_t(b_i, hband[:, :hi])
                - dot_t(hb_i, band[:, :hi])
            ) * scale
            r_id = lax.broadcasted_iota(jnp.int32, (TILE, TILE), 0)
            c_id = lax.broadcasted_iota(jnp.int32, (TILE, TILE), 1)
            square_r = real[:, :TILE]
            square_i = imag[:, lo:hi]
            diag = jnp.sum(jnp.where(r_id == c_id, square_r, 0.0), axis=0, keepdims=True)
            diag = jnp.broadcast_to(diag, (8, TILE))
            mixed = jnp.where(r_id < c_id, square_r, jnp.where(r_id > c_id, square_i, 0.0))
            pieces = [(lo, hi, mixed)]
            if lo > 0:
                pieces.append((0, lo, imag[:, :lo]))
            if hi < half:
                pieces.append((hi, half, real[:, TILE:]))
            for c0, c1, value in pieces:
                if first:
                    packed[lo:hi, c0:c1] = value
                else:
                    packed[lo:hi, c0:c1] = packed[lo:hi, c0:c1] + value
            if first:
                dl[:, lo:hi] = diag
            else:
                dl[:, lo:hi] = dl[:, lo:hi] + diag

    project(bands_ref.at[core], hbands_ref.at[core], True)
    swap_b.wait()
    swap_h.wait()
    project(rb, rh, False)

    far = LINE - 1
    q_far = lax.rem(z + far, LINE)
    direct = []
    for n, xx in enumerate((x, 1 - x)):
        zs[far - 1 + n] = packed[piece(q_far, xx), :].astype(jnp.bfloat16)
        copy = remote(
            zs.at[far - 1 + n],
            zr.at[far - 1 + n],
            zs_sem.at[far - 1 + n],
            zr_sem.at[far - 1 + n],
            device(q_far * 2 + xx, core),
        )
        if n == 0:
            copy.start()
        direct.append(copy)
    swaps = {}
    for d in (2, 1, 0):
        q = lax.rem(z + d, LINE)
        xs[d] = packed[piece(q, 1 - x), :].astype(jnp.bfloat16)
        swaps[d] = remote(xs.at[d], xr.at[d], xs_sem.at[d], xr_sem.at[d], across)
        swaps[d].start()
        if d == 2:
            direct[1].start()
    traces = []
    for r in range(1, CHIPS):
        copy = remote(
            dl,
            dr.at[r - 1],
            ds_sem.at[r - 1],
            dr_sem.at[r - 1],
            device(lax.rem(chip + r, CHIPS), core),
        )
        copy.start()
        traces.append(copy)
    sums = list(direct)
    for d in (2, 1):
        q = lax.rem(z + d, LINE)
        swaps[d].wait()
        zs[d - 1] = (packed[piece(q, x), :] + xr[d].astype(jnp.float32)).astype(jnp.bfloat16)
        copy = remote(
            zs.at[d - 1], zr.at[d - 1], zs_sem.at[d - 1], zr_sem.at[d - 1], device(q * 2 + x, core)
        )
        copy.start()
        sums.append(copy)
    swaps[0].wait()
    mine = packed[piece(z, x), :] + xr[0].astype(jnp.float32)
    for n, copy in zip((2, 3, 1, 0), sums):
        copy.wait()
        mine = mine + zr[n].astype(jnp.float32)
    own = piece(z, x)
    full[own, :] = mine.astype(jnp.bfloat16)

    def spread_own(n, target):
        return remote(full.at[own, :], full.at[own, :], gzs_sem.at[n], gzr_sem.at[n], target)

    passes = [remote(full.at[own, :], full.at[own, :], gxs_sem.at[0], gxr_sem.at[0], across)]
    passes[0].start()
    gathers = {}
    for d in (2, 1):
        gathers[d] = spread_own(d - 1, device(lax.rem(z + d, LINE) * 2 + x, core))
        gathers[d].start()
    for n, xx in enumerate((x, 1 - x)):
        gathers[far + n] = spread_own(far - 1 + n, device(q_far * 2 + xx, core))
        gathers[far + n].start()
    for d in (2, 1):
        gathers[d].wait_recv()
        theirs = piece(lax.rem(z - d + LINE, LINE), x)
        copy = remote(full.at[theirs, :], full.at[theirs, :], gxs_sem.at[d], gxr_sem.at[d], across)
        copy.start()
        passes.append(copy)
    diag = dl[...]
    for r in range(1, CHIPS):
        traces[r - 1].wait()
        diag = diag + dr[r - 1]
    diag = diag[0:1, :]
    for d in (2, 1):
        gathers[d].wait_send()
    for n in (0, 1):
        gathers[far + n].wait()
    for copy in passes:
        copy.wait()

    level = jnp.sum(diag, axis=1, keepdims=True) / half
    centred = diag - level
    total = jnp.sum(centred * centred, axis=1, keepdims=True)
    square_sum = jnp.zeros((1, half), jnp.float32)
    for i in range(tiles):
        block = full[i * TILE : (i + 1) * TILE, :].astype(jnp.float32)
        square_sum = square_sum + jnp.sum(block * block, axis=0, keepdims=True)
    total = total + 2.0 * jnp.sum(square_sum, axis=1, keepdims=True)
    spread = jnp.sqrt(total / half + 1e-06)
    factor = 1.0 / (4.0 * spread)
    filling = occ_ref[core].astype(jnp.float32) / half
    on_diag = filling - centred * factor
    for i in range(tiles):
        rows_i = slice(i * TILE, (i + 1) * TILE)
        r_id = lax.broadcasted_iota(jnp.int32, (TILE, TILE), 0)
        c_id = lax.broadcasted_iota(jnp.int32, (TILE, TILE), 1)
        block = full[rows_i, rows_i].astype(jnp.float32) * factor
        turned = block.T
        re0[rows_i, rows_i] = jnp.where(
            r_id == c_id, on_diag[:, rows_i], jnp.where(r_id < c_id, -block, -turned)
        ).astype(jnp.bfloat16)
        im0[rows_i, rows_i] = jnp.where(r_id > c_id, -block, turned).astype(jnp.bfloat16)
        for j in range(i + 1, tiles):
            rows_j = slice(j * TILE, (j + 1) * TILE)
            upper = full[rows_i, rows_j].astype(jnp.float32) * factor
            lower = full[rows_j, rows_i].astype(jnp.float32) * factor
            re0[rows_i, rows_j] = (-upper).astype(jnp.bfloat16)
            re0[rows_j, rows_i] = (-upper.T).astype(jnp.bfloat16)
            im0[rows_j, rows_i] = (-lower).astype(jnp.bfloat16)
            im0[rows_i, rows_j] = lower.T.astype(jnp.bfloat16)

    def purify(re, im, re_next, im_next):
        for i in range(tiles):
            lo = i * TILE
            own_rows = slice(lo, lo + TILE)
            right = slice(lo, half)
            r_i, i_i = re[own_rows, :], im[own_rows, :]
            re_c, im_c = re[:, right], im[:, right]
            sq_r = dot(r_i, re_c) - dot(i_i, im_c)
            sq_i = dot(r_i, im_c) + dot(i_i, re_c)
            sr[own_rows, right] = sq_r.astype(jnp.bfloat16)
            si[own_rows, right] = sq_i.astype(jnp.bfloat16)
            for k in range(1, tiles - i):
                part = slice(k * TILE, (k + 1) * TILE)
                below = slice(lo + k * TILE, lo + (k + 1) * TILE)
                sr[below, own_rows] = sq_r[:, part].T.astype(jnp.bfloat16)
                si[below, own_rows] = (-sq_i[:, part].T).astype(jnp.bfloat16)
            s_r, s_i = sr[own_rows, :], si[own_rows, :]
            new_r = 3.0 * sq_r - 2.0 * (dot(s_r, re_c) - dot(s_i, im_c))
            new_i = 3.0 * sq_i - 2.0 * (dot(s_r, im_c) + dot(s_i, re_c))
            re_next[own_rows, right] = new_r.astype(jnp.bfloat16)
            im_next[own_rows, right] = new_i.astype(jnp.bfloat16)
            for k in range(1, tiles - i):
                part = slice(k * TILE, (k + 1) * TILE)
                below = slice(lo + k * TILE, lo + (k + 1) * TILE)
                re_next[below, own_rows] = new_r[:, part].T.astype(jnp.bfloat16)
                im_next[below, own_rows] = (-new_i[:, part].T).astype(jnp.bfloat16)

    bufs = [(re0, im0), (re1, im1)]
    for step in range(MCW):
        purify(*bufs[step % 2], *bufs[(step + 1) % 2])
    re, im = bufs[MCW % 2]

    def update(band, target):
        a, b = band[:, :half], band[:, half:]
        target[:, :half] = (dot(a, re[...]) - dot(b, im[...])).astype(jnp.bfloat16)
        target[:, half:] = (dot(a, im[...]) + dot(b, re[...])).astype(jnp.bfloat16)

    update(rb, ob)
    back = remote(ob, out_ref.at[core], o_sem.at[0], o_sem.at[1], mate)
    back.start()
    update(bands_ref.at[core], out_ref.at[core])
    back.wait()


def fused(bands, hbands, occupied):
    points, rows, columns = bands.shape
    half = columns // 2
    share = half // CHIPS
    scale = 1.0 / (2.0 * rows * lax.axis_size("grid"))
    bf16, f32 = jnp.bfloat16, jnp.float32
    dma = pltpu.SemaphoreType.DMA
    return pl.pallas_call(
        functools.partial(kernel, scale),
        out_shape=jax.ShapeDtypeStruct(bands.shape, bf16),
        in_specs=[
            pl.BlockSpec(memory_space=pltpu.SMEM),
            pl.BlockSpec(memory_space=pltpu.VMEM),
            pl.BlockSpec(memory_space=pltpu.VMEM),
        ],
        out_specs=pl.BlockSpec(memory_space=pltpu.VMEM),
        scratch_shapes=[
            pltpu.VMEM((rows, columns), bf16),
            pltpu.VMEM((rows, columns), bf16),
            pltpu.VMEM((half, half), f32),
            pltpu.VMEM((LINE, share, half), bf16),
            pltpu.VMEM((LINE, share, half), bf16),
            pltpu.VMEM((LINE, share, half), bf16),
            pltpu.VMEM((LINE, share, half), bf16),
            pltpu.VMEM((8, half), f32),
            pltpu.VMEM((CHIPS - 1, 8, half), f32),
            pltpu.VMEM((half, half), bf16),
            pltpu.VMEM((half, half), bf16),
            pltpu.VMEM((half, half), bf16),
            pltpu.VMEM((half, half), bf16),
            pltpu.VMEM((half, half), bf16),
            pltpu.VMEM((half, half), bf16),
            pltpu.VMEM((half, half), bf16),
            pltpu.VMEM((rows, columns), bf16),
            dma((2,)),
            dma((2,)),
            dma((LINE,)),
            dma((LINE,)),
            dma((LINE,)),
            dma((LINE,)),
            dma((CHIPS - 1,)),
            dma((CHIPS - 1,)),
            dma((LINE,)),
            dma((LINE,)),
            dma((LINE,)),
            dma((LINE,)),
            dma((2,)),
        ],
        compiler_params=pltpu.CompilerParams(
            collective_id=0, has_side_effects=True, vmem_limit_bytes=50 * 1024 * 1024
        ),
    )(occupied, bands, hbands)


def embedding(full):
    width = full.shape[-1] // 2
    real_part = full[..., :width]
    imag_part = full[..., width:]
    upper = jnp.concatenate([real_part, imag_part], -1)
    lower = jnp.concatenate([-imag_part, real_part], -1)
    return jnp.concatenate([upper, lower], -2)


def spread_out(bands, hbands, occupied):
    points, local_rows, columns = bands.shape
    half = columns // 2
    devices = lax.axis_size("grid")
    share = half // devices
    scale = 1.0 / (2.0 * local_rows * devices)
    blocks = []
    for point in range(points):
        start = jnp.int32(0)
        count = lax.axis_size("grid") * share
        band_k = bands[point]
        hband_k = hbands[point]
        band_cols = jnp.concatenate(
            [
                lax.dynamic_slice_in_dim(band_k, start, count, 1),
                lax.dynamic_slice_in_dim(band_k, half, count, 1),
            ],
            1,
        )
        summed = jnp.einsum("gi,gj->ij", band_cols, hband_k, preferred_element_type=jnp.float32)
        hband_cols = jnp.concatenate(
            [
                lax.dynamic_slice_in_dim(hband_k, start, count, 1),
                lax.dynamic_slice_in_dim(hband_k, half, count, 1),
            ],
            1,
        )
        summed = summed + jnp.einsum(
            "gi,gj->ij", hband_cols, band_k, preferred_element_type=jnp.float32
        )
        real_rows = (summed[:count, :half] + summed[count:, half:]) * scale
        imag_rows = (summed[:count, half:] - summed[count:, :half]) * scale
        blocks.append(
            lax.psum_scatter(
                jnp.concatenate([real_rows, imag_rows], 1), "grid", scatter_dimension=0, tiled=True
            )
        )
    hamiltonian = jnp.stack(blocks, 1)
    hamiltonian = jnp.transpose(hamiltonian, (1, 0, 2))
    ham_real = hamiltonian[:, :, :half]
    ham_imag = hamiltonian[:, :, half:]
    row_index = lax.axis_index("grid") * share + lax.iota(jnp.int32, share)
    col_index = lax.iota(jnp.int32, half)
    identity = (row_index[:, None] == col_index[None, :]).astype(jnp.float32)[None]
    trace_part = jnp.sum(ham_real * identity, axis=(1, 2))
    trace = lax.psum(trace_part, "grid")
    level = (trace / half)[:, None, None]
    centred = ham_real - level * identity
    squares = jnp.sum(centred * centred, axis=(1, 2)) + jnp.sum(ham_imag * ham_imag, axis=(1, 2))
    total = lax.psum(squares, "grid")
    spread = jnp.sqrt(total / half + 1e-06)[:, None, None]
    filling = (occupied.astype(jnp.float32) / half)[:, None, None]
    dens_real = filling * identity - centred / (4.0 * spread)
    dens_imag = -ham_imag / (4.0 * spread)
    density = jnp.concatenate([dens_real, dens_imag], 2).astype(jnp.bfloat16)
    for repeat in range(MCW):
        gathered = lax.all_gather(density, "grid", axis=1, tiled=True)
        matrix = embedding(gathered)
        square = jnp.einsum("krc,kcd->krd", density, matrix, preferred_element_type=jnp.float32)
        cube = jnp.einsum(
            "krc,kcd->krd", square.astype(jnp.bfloat16), matrix, preferred_element_type=jnp.float32
        )
        density = (3.0 * square - 2.0 * cube).astype(jnp.bfloat16)
    gathered = lax.all_gather(density, "grid", axis=1, tiled=True)
    matrix = embedding(gathered)
    updated = jnp.einsum("kgc,kcd->kgd", bands, matrix, preferred_element_type=jnp.float32)
    return updated.astype(jnp.bfloat16)


def on_device(bands, hbands, occupied):
    points, rows, columns = bands.shape
    half = columns // 2
    if (
        lax.axis_size("grid") == 2 * CHIPS
        and points == 2
        and half % TILE == 0
        and half % (16 * CHIPS) == 0
    ):
        return fused(bands, hbands, occupied)
    return spread_out(bands, hbands, occupied)


def solution(mesh):
    return jax.shard_map(
        on_device,
        mesh=mesh,
        in_specs=(P("kset", "grid", None), P("kset", "grid", None), P("kset")),
        out_specs=P("kset", "grid", None),
        check_vma=False,
    )
```

```python
import functools

import jax
import jax.numpy as jnp
from jax import lax
from jax.experimental import pallas as pl
from jax.experimental.pallas import tpu as pltpu
from jax.sharding import PartitionSpec as P

MCW = 2
LINE = 4
CHIPS = 2 * LINE
TILE = 256
MESH = pl.DeviceIdType.MESH


def dot_t(left, right):
    return lax.dot_general(
        left, right, (((0,), (0,)), ((), ())), preferred_element_type=jnp.float32
    )


def dot(left, right):
    return jnp.dot(left, right, preferred_element_type=jnp.float32)


def kernel(
    scale,
    occ_ref,
    bands_ref,
    hbands_ref,
    out_ref,
    mb,
    mh,
    rb,
    rh,
    packed,
    xs,
    xr,
    zs,
    zr,
    dl,
    dr,
    full,
    re0,
    im0,
    re1,
    im1,
    sr,
    si,
    ob,
    in_send,
    in_recv,
    xs_sem,
    xr_sem,
    zs_sem,
    zr_sem,
    ds_sem,
    dr_sem,
    gzs_sem,
    gzr_sem,
    gxs_sem,
    gxr_sem,
    o_sem,
    load_sem,
):
    rows = bands_ref.shape[1]
    half = bands_ref.shape[2] // 2
    share = half // CHIPS
    tiles = half // TILE
    kset = lax.axis_index("kset")
    me = lax.axis_index("grid")
    core = lax.rem(me, 2)
    chip = me // 2
    x = lax.rem(chip, 2)
    z = chip // 2

    def device(chip_id, core_id):
        return (kset, chip_id * 2 + core_id)

    mate = device(chip, 1 - core)
    across = device(z * 2 + 1 - x, core)

    def piece(zz, xx):
        return pl.ds(pl.multiple_of((zz * 2 + xx) * share, 16), share)

    def remote(src, dst, send, recv, target):
        return pltpu.make_async_remote_copy(
            src_ref=src,
            dst_ref=dst,
            send_sem=send,
            recv_sem=recv,
            device_id=target,
            device_id_type=MESH,
        )

    load_b = pltpu.make_async_copy(bands_ref.at[core], mb, load_sem.at[0])
    load_h = pltpu.make_async_copy(hbands_ref.at[core], mh, load_sem.at[1])
    load_b.start()
    load_h.start()
    barrier = pltpu.get_barrier_semaphore()
    pl.semaphore_signal(barrier, inc=1, device_id=mate, device_id_type=MESH)
    for r in range(1, CHIPS):
        pl.semaphore_signal(
            barrier, inc=1, device_id=device(lax.rem(chip + r, CHIPS), core), device_id_type=MESH
        )
    pl.semaphore_wait(barrier, CHIPS)

    swap_b = remote(bands_ref.at[1 - core], rb, in_send.at[0], in_recv.at[0], mate)
    swap_h = remote(hbands_ref.at[1 - core], rh, in_send.at[1], in_recv.at[1], mate)
    swap_b.start()
    swap_h.start()

    def project(band, hband, first):
        for i in range(tiles):
            lo, hi = i * TILE, (i + 1) * TILE
            a_i = band[:, lo:hi]
            b_i = band[:, half + lo : half + hi]
            ha_i = hband[:, lo:hi]
            hb_i = hband[:, half + lo : half + hi]
            real = (
                dot_t(a_i, hband[:, lo:half])
                + dot_t(b_i, hband[:, half + lo :])
                + dot_t(ha_i, band[:, lo:half])
                + dot_t(hb_i, band[:, half + lo :])
            ) * scale
            imag = (
                dot_t(a_i, hband[:, half : half + hi])
                + dot_t(ha_i, band[:, half : half + hi])
                - dot_t(b_i, hband[:, :hi])
                - dot_t(hb_i, band[:, :hi])
            ) * scale
            r_id = lax.broadcasted_iota(jnp.int32, (TILE, TILE), 0)
            c_id = lax.broadcasted_iota(jnp.int32, (TILE, TILE), 1)
            square_r = real[:, :TILE]
            square_i = imag[:, lo:hi]
            diag = jnp.sum(jnp.where(r_id == c_id, square_r, 0.0), axis=0, keepdims=True)
            mixed = jnp.where(r_id < c_id, square_r, jnp.where(r_id > c_id, square_i, 0.0))
            pieces = [(lo, hi, mixed)]
            if lo > 0:
                pieces.append((0, lo, imag[:, :lo]))
            if hi < half:
                pieces.append((hi, half, real[:, TILE:]))
            for c0, c1, value in pieces:
                if first:
                    packed[lo:hi, c0:c1] = value
                else:
                    packed[lo:hi, c0:c1] = packed[lo:hi, c0:c1] + value
            if first:
                dl[:, lo:hi] = diag
            else:
                dl[:, lo:hi] = dl[:, lo:hi] + diag

    load_b.wait()
    load_h.wait()
    project(mb, mh, True)
    swap_b.wait()
    swap_h.wait()
    project(rb, rh, False)

    far = LINE - 1
    q_far = lax.rem(z + far, LINE)
    direct = []
    for n, xx in enumerate((x, 1 - x)):
        zs[far - 1 + n] = packed[piece(q_far, xx), :].astype(jnp.bfloat16)
        copy = remote(
            zs.at[far - 1 + n],
            zr.at[far - 1 + n],
            zs_sem.at[far - 1 + n],
            zr_sem.at[far - 1 + n],
            device(q_far * 2 + xx, core),
        )
        if n == 0:
            copy.start()
        direct.append(copy)
    swaps = {}
    for d in (2, 1, 0):
        q = lax.rem(z + d, LINE)
        xs[d] = packed[piece(q, 1 - x), :].astype(jnp.bfloat16)
        swaps[d] = remote(xs.at[d], xr.at[d], xs_sem.at[d], xr_sem.at[d], across)
        swaps[d].start()
        if d == 2:
            direct[1].start()
    traces = []
    for r in range(1, CHIPS):
        copy = remote(
            dl,
            dr.at[r - 1],
            ds_sem.at[r - 1],
            dr_sem.at[r - 1],
            device(lax.rem(chip + r, CHIPS), core),
        )
        copy.start()
        traces.append(copy)
    sums = list(direct)
    for d in (2, 1):
        q = lax.rem(z + d, LINE)
        swaps[d].wait()
        zs[d - 1] = (packed[piece(q, x), :] + xr[d].astype(jnp.float32)).astype(jnp.bfloat16)
        copy = remote(
            zs.at[d - 1], zr.at[d - 1], zs_sem.at[d - 1], zr_sem.at[d - 1], device(q * 2 + x, core)
        )
        copy.start()
        sums.append(copy)
    swaps[0].wait()
    mine = packed[piece(z, x), :] + xr[0].astype(jnp.float32)
    for n, copy in zip((2, 3, 1, 0), sums):
        copy.wait()
        mine = mine + zr[n].astype(jnp.float32)
    own = piece(z, x)
    full[own, :] = mine.astype(jnp.bfloat16)

    def spread_own(n, target):
        return remote(full.at[own, :], full.at[own, :], gzs_sem.at[n], gzr_sem.at[n], target)

    passes = [remote(full.at[own, :], full.at[own, :], gxs_sem.at[0], gxr_sem.at[0], across)]
    passes[0].start()
    gathers = {}
    for d in (2, 1):
        gathers[d] = spread_own(d - 1, device(lax.rem(z + d, LINE) * 2 + x, core))
        gathers[d].start()
    for n, xx in enumerate((x, 1 - x)):
        gathers[far + n] = spread_own(far - 1 + n, device(q_far * 2 + xx, core))
        gathers[far + n].start()
    for d in (2, 1):
        gathers[d].wait_recv()
        theirs = piece(lax.rem(z - d + LINE, LINE), x)
        copy = remote(full.at[theirs, :], full.at[theirs, :], gxs_sem.at[d], gxr_sem.at[d], across)
        copy.start()
        passes.append(copy)
    diag = dl[...]
    for r in range(1, CHIPS):
        traces[r - 1].wait()
        diag = diag + dr[r - 1]
    for d in (2, 1):
        gathers[d].wait_send()
    for n in (0, 1):
        gathers[far + n].wait()
    for copy in passes:
        copy.wait()

    level = jnp.sum(diag, axis=1, keepdims=True) / half
    centred = diag - level
    total = jnp.sum(centred * centred, axis=1, keepdims=True)
    square_sum = jnp.zeros((1, half), jnp.float32)
    for i in range(tiles):
        block = full[i * TILE : (i + 1) * TILE, :].astype(jnp.float32)
        square_sum = square_sum + jnp.sum(block * block, axis=0, keepdims=True)
    total = total + 2.0 * jnp.sum(square_sum, axis=1, keepdims=True)
    spread = jnp.sqrt(total / half + 1e-06)
    factor = 1.0 / (4.0 * spread)
    filling = occ_ref[core].astype(jnp.float32) / half
    on_diag = filling - centred * factor
    for i in range(tiles):
        rows_i = slice(i * TILE, (i + 1) * TILE)
        r_id = lax.broadcasted_iota(jnp.int32, (TILE, TILE), 0)
        c_id = lax.broadcasted_iota(jnp.int32, (TILE, TILE), 1)
        block = full[rows_i, rows_i].astype(jnp.float32) * factor
        turned = block.T
        re0[rows_i, rows_i] = jnp.where(
            r_id == c_id, on_diag[:, rows_i], jnp.where(r_id < c_id, -block, -turned)
        ).astype(jnp.bfloat16)
        im0[rows_i, rows_i] = jnp.where(r_id > c_id, -block, turned).astype(jnp.bfloat16)
        for j in range(i + 1, tiles):
            rows_j = slice(j * TILE, (j + 1) * TILE)
            upper = full[rows_i, rows_j].astype(jnp.float32) * factor
            lower = full[rows_j, rows_i].astype(jnp.float32) * factor
            re0[rows_i, rows_j] = (-upper).astype(jnp.bfloat16)
            re0[rows_j, rows_i] = (-upper.T).astype(jnp.bfloat16)
            im0[rows_j, rows_i] = (-lower).astype(jnp.bfloat16)
            im0[rows_i, rows_j] = lower.T.astype(jnp.bfloat16)

    def purify(re, im, re_next, im_next):
        for i in range(tiles):
            lo = i * TILE
            own_rows = slice(lo, lo + TILE)
            right = slice(lo, half)
            r_i, i_i = re[own_rows, :], im[own_rows, :]
            re_c, im_c = re[:, right], im[:, right]
            sq_r = dot(r_i, re_c) - dot(i_i, im_c)
            sq_i = dot(r_i, im_c) + dot(i_i, re_c)
            sr[own_rows, right] = sq_r.astype(jnp.bfloat16)
            si[own_rows, right] = sq_i.astype(jnp.bfloat16)
            for k in range(1, tiles - i):
                part = slice(k * TILE, (k + 1) * TILE)
                below = slice(lo + k * TILE, lo + (k + 1) * TILE)
                sr[below, own_rows] = sq_r[:, part].T.astype(jnp.bfloat16)
                si[below, own_rows] = (-sq_i[:, part].T).astype(jnp.bfloat16)
            s_r, s_i = sr[own_rows, :], si[own_rows, :]
            new_r = 3.0 * sq_r - 2.0 * (dot(s_r, re_c) - dot(s_i, im_c))
            new_i = 3.0 * sq_i - 2.0 * (dot(s_r, im_c) + dot(s_i, re_c))
            re_next[own_rows, right] = new_r.astype(jnp.bfloat16)
            im_next[own_rows, right] = new_i.astype(jnp.bfloat16)
            for k in range(1, tiles - i):
                part = slice(k * TILE, (k + 1) * TILE)
                below = slice(lo + k * TILE, lo + (k + 1) * TILE)
                re_next[below, own_rows] = new_r[:, part].T.astype(jnp.bfloat16)
                im_next[below, own_rows] = (-new_i[:, part].T).astype(jnp.bfloat16)

    bufs = [(re0, im0), (re1, im1)]
    for step in range(MCW):
        purify(*bufs[step % 2], *bufs[(step + 1) % 2])
    re, im = bufs[MCW % 2]

    def update(band, target):
        a, b = band[:, :half], band[:, half:]
        target[:, :half] = (dot(a, re[...]) - dot(b, im[...])).astype(jnp.bfloat16)
        target[:, half:] = (dot(a, im[...]) + dot(b, re[...])).astype(jnp.bfloat16)

    update(rb, ob)
    back = remote(ob, out_ref.at[core], o_sem.at[0], o_sem.at[1], mate)
    back.start()
    update(mb, out_ref.at[core])
    back.wait()


def fused(bands, hbands, occupied):
    points, rows, columns = bands.shape
    half = columns // 2
    share = half // CHIPS
    scale = 1.0 / (2.0 * rows * lax.axis_size("grid"))
    bf16, f32 = jnp.bfloat16, jnp.float32
    dma = pltpu.SemaphoreType.DMA
    return pl.pallas_call(
        functools.partial(kernel, scale),
        out_shape=jax.ShapeDtypeStruct(bands.shape, bf16),
        in_specs=[
            pl.BlockSpec(memory_space=pltpu.SMEM),
            pl.BlockSpec(memory_space=pltpu.HBM),
            pl.BlockSpec(memory_space=pltpu.HBM),
        ],
        out_specs=pl.BlockSpec(memory_space=pltpu.VMEM),
        scratch_shapes=[
            pltpu.VMEM((rows, columns), bf16),
            pltpu.VMEM((rows, columns), bf16),
            pltpu.VMEM((rows, columns), bf16),
            pltpu.VMEM((rows, columns), bf16),
            pltpu.VMEM((half, half), f32),
            pltpu.VMEM((LINE, share, half), bf16),
            pltpu.VMEM((LINE, share, half), bf16),
            pltpu.VMEM((LINE, share, half), bf16),
            pltpu.VMEM((LINE, share, half), bf16),
            pltpu.VMEM((1, half), f32),
            pltpu.VMEM((CHIPS - 1, 1, half), f32),
            pltpu.VMEM((half, half), bf16),
            pltpu.VMEM((half, half), bf16),
            pltpu.VMEM((half, half), bf16),
            pltpu.VMEM((half, half), bf16),
            pltpu.VMEM((half, half), bf16),
            pltpu.VMEM((half, half), bf16),
            pltpu.VMEM((half, half), bf16),
            pltpu.VMEM((rows, columns), bf16),
            dma((2,)),
            dma((2,)),
            dma((LINE,)),
            dma((LINE,)),
            dma((LINE,)),
            dma((LINE,)),
            dma((CHIPS - 1,)),
            dma((CHIPS - 1,)),
            dma((LINE,)),
            dma((LINE,)),
            dma((LINE,)),
            dma((LINE,)),
            dma((2,)),
            dma((2,)),
        ],
        compiler_params=pltpu.CompilerParams(
            collective_id=0, has_side_effects=True, vmem_limit_bytes=61 * 1024 * 1024
        ),
    )(occupied, bands, hbands)


def embedding(full):
    width = full.shape[-1] // 2
    real_part = full[..., :width]
    imag_part = full[..., width:]
    upper = jnp.concatenate([real_part, imag_part], -1)
    lower = jnp.concatenate([-imag_part, real_part], -1)
    return jnp.concatenate([upper, lower], -2)


def spread_out(bands, hbands, occupied):
    points, local_rows, columns = bands.shape
    half = columns // 2
    devices = lax.axis_size("grid")
    share = half // devices
    scale = 1.0 / (2.0 * local_rows * devices)
    blocks = []
    for point in range(points):
        start = jnp.int32(0)
        count = lax.axis_size("grid") * share
        band_k = bands[point]
        hband_k = hbands[point]
        band_cols = jnp.concatenate(
            [
                lax.dynamic_slice_in_dim(band_k, start, count, 1),
                lax.dynamic_slice_in_dim(band_k, half, count, 1),
            ],
            1,
        )
        summed = jnp.einsum("gi,gj->ij", band_cols, hband_k, preferred_element_type=jnp.float32)
        hband_cols = jnp.concatenate(
            [
                lax.dynamic_slice_in_dim(hband_k, start, count, 1),
                lax.dynamic_slice_in_dim(hband_k, half, count, 1),
            ],
            1,
        )
        summed = summed + jnp.einsum(
            "gi,gj->ij", hband_cols, band_k, preferred_element_type=jnp.float32
        )
        real_rows = (summed[:count, :half] + summed[count:, half:]) * scale
        imag_rows = (summed[:count, half:] - summed[count:, :half]) * scale
        blocks.append(
            lax.psum_scatter(
                jnp.concatenate([real_rows, imag_rows], 1), "grid", scatter_dimension=0, tiled=True
            )
        )
    hamiltonian = jnp.stack(blocks, 1)
    hamiltonian = jnp.transpose(hamiltonian, (1, 0, 2))
    ham_real = hamiltonian[:, :, :half]
    ham_imag = hamiltonian[:, :, half:]
    row_index = lax.axis_index("grid") * share + lax.iota(jnp.int32, share)
    col_index = lax.iota(jnp.int32, half)
    identity = (row_index[:, None] == col_index[None, :]).astype(jnp.float32)[None]
    trace_part = jnp.sum(ham_real * identity, axis=(1, 2))
    trace = lax.psum(trace_part, "grid")
    level = (trace / half)[:, None, None]
    centred = ham_real - level * identity
    squares = jnp.sum(centred * centred, axis=(1, 2)) + jnp.sum(ham_imag * ham_imag, axis=(1, 2))
    total = lax.psum(squares, "grid")
    spread = jnp.sqrt(total / half + 1e-06)[:, None, None]
    filling = (occupied.astype(jnp.float32) / half)[:, None, None]
    dens_real = filling * identity - centred / (4.0 * spread)
    dens_imag = -ham_imag / (4.0 * spread)
    density = jnp.concatenate([dens_real, dens_imag], 2).astype(jnp.bfloat16)
    for repeat in range(MCW):
        gathered = lax.all_gather(density, "grid", axis=1, tiled=True)
        matrix = embedding(gathered)
        square = jnp.einsum("krc,kcd->krd", density, matrix, preferred_element_type=jnp.float32)
        cube = jnp.einsum(
            "krc,kcd->krd", square.astype(jnp.bfloat16), matrix, preferred_element_type=jnp.float32
        )
        density = (3.0 * square - 2.0 * cube).astype(jnp.bfloat16)
    gathered = lax.all_gather(density, "grid", axis=1, tiled=True)
    matrix = embedding(gathered)
    updated = jnp.einsum("kgc,kcd->kgd", bands, matrix, preferred_element_type=jnp.float32)
    return updated.astype(jnp.bfloat16)


def on_device(bands, hbands, occupied):
    points, rows, columns = bands.shape
    half = columns // 2
    if (
        lax.axis_size("grid") == 2 * CHIPS
        and points == 2
        and half % TILE == 0
        and half % (16 * CHIPS) == 0
    ):
        return fused(bands, hbands, occupied)
    return spread_out(bands, hbands, occupied)


def solution(mesh):
    return jax.shard_map(
        on_device,
        mesh=mesh,
        in_specs=(P("kset", "grid", None), P("kset", "grid", None), P("kset")),
        out_specs=P("kset", "grid", None),
        check_vma=False,
    )
```
